32 devices in a mesh: freq: 4 (over x, core), grid: 8 (over z, y).
Axes of the slice: x: 2, y: 2, z: 4, core: 2. Of those that a mesh axis runs over, the one named last changes fastest.
Arguments:
- series: bfloat16 [128, 1024, 256], P('freq', 'grid'), may hold values from -8 to 8
- bins: int32 [4], replicated, may hold values from 32 to 127
- sensor_coords: int32 [3, 1024], replicated, may hold values from 0 to 63
- grid_coords: int32 [3, 2048], P(None, 'grid'), may hold values from 0 to 63
Outputs:
- bin_power: float32 [4, 2048], P('freq', 'grid')
- power: float32 [2048], P('grid')
The draws below stay inside these ranges and needn't reach their ends.
All inputs are finite; a program needn't handle non-finite values.
Results may differ from the reference program's by a relative error of at most 0.0015.
Values may be sent and summed in bfloat16 or wider, within the bound.
No kernel may reach another device: no remote copies, remote signals or barrier semaphores. Data moves between devices by JAX's collectives and lax.ppermute only.
A program may use at most 64 MiB of HBM per device.

```python
import math
import jax
import jax.numpy as jnp
from jax import lax

CH = 1024
SAMP = 256
COORD = 64
NF = 4
SNAPS = 128
GRID = 2048


def draw_series(key, part):
    keys = jax.random.split(jax.random.fold_in(key, 11), 4)
    loud = 16
    lowest, highest = (0.12, 0.4)
    noise = jax.random.normal(keys[0], (SNAPS, CH, SAMP), jnp.float32)
    waves = jax.random.normal(keys[1], (SNAPS, loud, SAMP), jnp.float32)
    mixing = jax.random.normal(keys[2], (CH, loud), jnp.float32)
    levels = jnp.exp(jax.random.uniform(keys[3], (loud,), jnp.float32, jnp.log(lowest), jnp.log(highest)))
    signal = jnp.einsum('skt,ck->sct', waves * levels[None, :, None], mixing)
    return jnp.clip((noise + signal) / 2.0, -8.0, 8.0).astype(jnp.bfloat16)


def touch_ends(result, stream_key, least, high):
    extent = result.shape
    index_at = [jax.random.randint(jax.random.fold_in(stream_key, axis), (), 0, extent[axis]) for axis in range(len(extent))]
    result = result.at[tuple(index_at)].set(least)
    longest = extent.index(max(extent))
    index_at[longest] = (index_at[longest] + 1) % extent[longest]
    return result.at[tuple(index_at)].set(high)


def setup_inputs(seed: int = 0) -> dict:
    streams_of = jax.random.split(jax.random.key(seed), 5)
    return {
        "series": draw_series(jax.random.fold_in(streams_of[4], 71), 0),
        "bins": touch_ends(jax.random.randint(streams_of[1], (NF,), SAMP // 8, SAMP // 2), jax.random.fold_in(streams_of[1], 1), SAMP // 8, (SAMP // 2) - 1).astype(jnp.int32),
        "sensor_coords": touch_ends(jax.random.randint(streams_of[2], (3, CH), 0, COORD), jax.random.fold_in(streams_of[2], 1), 0, COORD - 1).astype(jnp.int32),
        "grid_coords": touch_ends(jax.random.randint(streams_of[3], (3, GRID), 0, COORD), jax.random.fold_in(streams_of[3], 1), 0, COORD - 1).astype(jnp.int32),
    }


def make_table(bins, samples):
    sample_index = jnp.arange(samples, dtype=jnp.int32)
    cycles = bins[:, None] * sample_index[None, :] % samples
    angles = 2.0 * math.pi / samples * cycles.astype(jnp.float32)
    scaling = (samples / 2.0) ** (-0.5)
    table = jnp.stack([jnp.cos(angles) * scaling, -jnp.sin(angles) * scaling], 1)
    return table.astype(jnp.bfloat16).reshape(2 * bins.shape[0], samples)

def reference(series, bins, sensor_coords, grid_coords):
    snap_total, channels, samples = series.shape
    table = make_table(bins, samples)
    flat = series.reshape(snap_total * channels, samples)
    spectra = jnp.dot(table, flat.T, preferred_element_type=jnp.float32)
    spectra = spectra.astype(jnp.bfloat16).reshape(2 * bins.shape[0], snap_total, channels)
    spectra = jnp.transpose(spectra, (0, 2, 1)).reshape(bins.shape[0], 2, channels, snap_total)
    squared = jnp.zeros((grid_coords.shape[1], channels), jnp.int32)
    for axis_pos in range(3):
        offsets = grid_coords[axis_pos][:, None] - sensor_coords[axis_pos][None, :]
        squared = squared + offsets * offsets
    distance = jnp.sqrt(squared.astype(jnp.float32))
    amplitude = channels ** (-0.5)

    def one_bin(item):
        bin_value, spec = item
        phases = 4.0 * math.pi / samples * bin_value.astype(jnp.float32) * distance
        beam_real = (jnp.cos(phases) * amplitude).astype(jnp.bfloat16).astype(jnp.float32)
        beam_imag = (-jnp.sin(phases) * amplitude).astype(jnp.bfloat16).astype(jnp.float32)
        spec_real = spec[0].astype(jnp.float32)
        spec_imag = spec[1].astype(jnp.float32)
        out_real = jnp.dot(beam_real, spec_real) + jnp.dot(beam_imag, spec_imag)
        out_imag = jnp.dot(beam_real, spec_imag) - jnp.dot(beam_imag, spec_real)
        return lax.optimization_barrier(jnp.sum(out_real * out_real + out_imag * out_imag, 1)) / snap_total
    bin_power = lax.map(one_bin, (bins, spectra))
    power = lax.optimization_barrier(jnp.sum(bin_power, 0)) / bins.shape[0]
    return (bin_power, power)
```

```python
import math

import jax
import jax.numpy as jnp
from jax import lax
from jax.sharding import PartitionSpec as P


def turns_cos_sin(turns):
    rest = turns - jnp.round(turns)
    x = rest * math.pi
    z = x * x
    s = x * (1.0 + z * (-1 / 6 + z * (1 / 120 + z * (-1 / 5040 + z * (1 / 362880 - z / 39916800)))))
    c = 1.0 + z * (-0.5 + z * (1 / 24 + z * (-1 / 720 + z * (1 / 40320 + z * (-1 / 3628800 + z / 479001600)))))
    return 1.0 - 2.0 * s * s, 2.0 * s * c


def on_device(series, bins, sensor_coords, grid_coords):
    snap_local, channel_local, samples = series.shape
    all_bins = bins.shape[0]
    channels = sensor_coords.shape[1]
    grid_local = grid_coords.shape[1]
    freq_size = lax.axis_size("freq")
    grid_size = lax.axis_size("grid")
    snap_total = snap_local * freq_size
    half = all_bins // 2
    place = lax.axis_index("grid")
    side = place % 2

    def swap(value, axis, mask):
        size = lax.axis_size(axis)
        return lax.ppermute(value, axis, [(i, i ^ mask) for i in range(size)])

    ordered = jnp.where(side == 0, bins, jnp.roll(bins, half))
    sample_index = jnp.arange(samples, dtype=jnp.int32)
    cycles = ordered[:, None] * sample_index[None, :] % samples
    angles = 2.0 * math.pi / samples * cycles.astype(jnp.float32)
    scaling = (samples / 2.0) ** (-0.5)
    table = jnp.stack([jnp.cos(angles) * scaling, -jnp.sin(angles) * scaling], 1)
    table = table.astype(jnp.bfloat16).reshape(2 * all_bins, samples)
    spectra = jnp.einsum("kt,sct->ksc", table, series, preferred_element_type=jnp.float32)
    spectra = spectra.astype(jnp.bfloat16).reshape(2 * all_bins * snap_local, channel_local)
    rows = all_bins * snap_local
    keep, send = spectra[:rows], spectra[rows:]
    points = grid_coords.astype(jnp.bfloat16).reshape(-1, channel_local)
    received = swap(jnp.concatenate([send, points], 0), "grid", 1)
    other_points = received[rows:].reshape(grid_coords.shape).astype(jnp.int32)
    pair = jnp.stack([keep, received[:rows]], 1)
    blocks = [pair] + [swap(pair, "grid", 2 * k) for k in range(1, grid_size // 2)]

    my_bins = ordered[:half].astype(jnp.float32)
    amplitude = channels ** (-0.5)
    sensors = sensor_coords.reshape(3, grid_size, channel_local)
    picks = jnp.arange(grid_size) ^ place
    sensors = sensors[:, picks].reshape(3, channels)
    beams = []
    for these in (grid_coords, other_points):
        squared = jnp.zeros((channels, grid_local), jnp.int32)
        for axis_pos in range(3):
            offsets = these[axis_pos][None, :] - sensors[axis_pos][:, None]
            squared = squared + offsets * offsets
        distance = jnp.sqrt(squared.astype(jnp.float32))
        turns = (2.0 / samples) * my_bins[:, None, None] * distance[None]
        cosine, sine = turns_cos_sin(turns)
        beam = ((cosine * amplitude).astype(jnp.bfloat16), (-sine * amplitude).astype(jnp.bfloat16))
        beams.append(lax.optimization_barrier(beam))
    partial = []
    for real, imag in beams:
        first = second = 0.0
        for k, block in enumerate(blocks):
            left = block.reshape(half, 2 * snap_local, 2 * channel_local)
            span = slice(2 * k * channel_local, 2 * (k + 1) * channel_local)
            first += jnp.einsum("fsc,fcg->fsg", left, real[:, span], preferred_element_type=jnp.float32)
            second += jnp.einsum("fsc,fcg->fsg", left, imag[:, span], preferred_element_type=jnp.float32)
        out_real = first[:, :snap_local] + second[:, snap_local:]
        out_imag = first[:, snap_local:] - second[:, :snap_local]
        partial.append(jnp.sum(out_real * out_real + out_imag * out_imag, 1))
    total = jnp.concatenate([partial[0], swap(partial[1], "grid", 1)], 0)
    step = freq_size // 2
    while step:
        total = total + swap(total, "freq", step)
        step //= 2
    total = total / snap_total
    bin_count = all_bins // freq_size
    mine = (lax.axis_index("freq") * bin_count + side * half) % all_bins
    bin_power = lax.dynamic_slice_in_dim(total, mine, bin_count)
    power = jnp.sum(total, 0) / all_bins
    return (bin_power, power)


def solution(mesh):
    return jax.shard_map(
        on_device,
        mesh=mesh,
        in_specs=(P("freq", "grid", None), P(), P(), P(None, "grid")),
        out_specs=(P("freq", "grid"), P("grid")),
        check_vma=False,
    )
```

```python
import functools
import math

import jax
import jax.numpy as jnp
from jax import lax
from jax.experimental import pallas as pl
from jax.experimental.pallas import tpu as pltpu
from jax.sharding import PartitionSpec as P


def fit(function, degree):
    import numpy as np

    nodes = 0.125 + 0.125 * np.cos(math.pi * (np.arange(degree + 1) + 0.5) / (degree + 1))
    matrix = np.vander(nodes, degree + 1, increasing=True)
    return [float(v) for v in np.linalg.solve(matrix, function(np.sqrt(nodes)))]


def fits():
    import numpy as np

    return fit(lambda x: np.sin(math.pi * x) / x, 5), fit(lambda x: np.cos(math.pi * x), 5)


def horner(u, coefficients):
    total = coefficients[-1]
    for value in coefficients[-2::-1]:
        total = total * u + value
    return total


def scaled_cos_sin(turns, scale):
    whole = (turns + 12582912.0) - 12582912.0
    x = turns - whole
    u = x * x
    sine, cosine = fits()
    root = math.sqrt(2.0 * scale)
    s = x * horner(u, [v * root for v in sine])
    c = horner(u, [-v * root for v in cosine])
    return scale - s * s, s * c


def transform_kernel(half, bins_far, points_far, series_ref, keep_ref, send_ref, bins_ref, points_ref, held, tall, sems, small_sems):
    side = lax.axis_index("grid") % 2
    snaps, channels, samples = held.shape
    rows = tall.shape[0] // snaps
    all_bins = rows // 2
    chunks = sems.shape[0]
    step = snaps // chunks
    copies = [
        pltpu.make_async_copy(series_ref.at[pl.ds(i * step, step)], held.at[pl.ds(i * step, step)], sems.at[i])
        for i in range(chunks)
    ]
    small = [
        pltpu.make_async_copy(bins_far, bins_ref, small_sems.at[0]),
        pltpu.make_async_copy(points_far, points_ref, small_sems.at[1]),
    ]
    for copy in small + copies:
        copy.start()
    for copy in small:
        copy.wait()
    row = lax.broadcasted_iota(jnp.int32, (rows, samples), 0)
    sample = lax.broadcasted_iota(jnp.int32, (rows, samples), 1)
    number = jnp.zeros((rows, samples), jnp.int32)
    for f in range(all_bins):
        number = jnp.where(row // 2 == f, bins_ref[(f + side * half) % all_bins], number)
    turns = (number * sample).astype(jnp.float32) * (1.0 / samples)
    cosine, sine = scaled_cos_sin(turns, (samples / 2.0) ** (-0.5))
    table = jnp.where(row % 2 == 0, cosine, sine).astype(jnp.bfloat16)
    group = 2 if channels % 128 == 0 and step % 2 == 0 else 1
    for i, copy in enumerate(copies):
        copy.wait()
        for s in range(i * step, (i + 1) * step, group):
            block = held[s : s + group].reshape(group * channels, samples)
            out = lax.dot_general(table, block, (((1,), (1,)), ((), ())), preferred_element_type=jnp.float32)
            for p in range(group):
                tall[pl.ds((s + p) * rows, rows), :] = out[:, p * channels : (p + 1) * channels]
    for k in range(rows):
        picked = tall[pl.ds(k, snaps, stride=rows), :].astype(jnp.bfloat16)
        target, base = (keep_ref, k) if k < rows // 2 else (send_ref, k - rows // 2)
        target[pl.ds(base * snaps, snaps), :] = picked
    extra = send_ref.shape[0] - rows // 2 * snaps
    pieces = [
        points_ref[pl.ds(a, 1), pl.ds(p, channels)].astype(jnp.float32)
        for a in range(points_ref.shape[0])
        for p in range(0, points_ref.shape[1], channels)
    ]
    pieces.append(jnp.zeros((extra - len(pieces), channels), jnp.float32))
    send_ref[pl.ds(rows // 2 * snaps, extra), :] = jnp.concatenate(pieces, 0).astype(jnp.bfloat16)


def pair_kernel(keep_ref, received_ref, pair_ref):
    side = lax.axis_index("grid") % 2
    rows, channels = keep_ref.shape

    @pl.when(side == 0)
    def _():
        pair_ref[:, :channels] = keep_ref[...]
        pair_ref[:, channels:] = received_ref[:rows, :]

    @pl.when(side == 1)
    def _():
        pair_ref[:, channels:] = keep_ref[...]
        pair_ref[:, :channels] = received_ref[:rows, :]


def split(value):
    high = jnp.floor(value * (1.0 / 64.0))
    return high, value - 64.0 * high


def replica_kernel(half, samples, packed, bins_ref, sensors_ref, points_ref, beam_ref, squares):
    side = lax.axis_index("grid") % 2
    channels = sensors_ref.shape[1]
    points = beam_ref.shape[3]
    sensors = [sensors_ref[pl.ds(a, 1), :].astype(jnp.float32) for a in range(3)]
    if packed:
        width = points_ref.shape[1]
        base = points_ref.shape[0] - packed
        tail = points_ref[pl.ds(base, packed), :].astype(jnp.float32)
        per = points // width
        places = [jnp.concatenate([tail[a * per + p : a * per + p + 1] for p in range(per)], 1) for a in range(3)]
    else:
        places = [points_ref[pl.ds(a, 1), :].astype(jnp.float32) for a in range(3)]
    s_high, s_low = split(sum(v * v for v in sensors))
    g_high, g_low = split(sum(v * v for v in places))
    one = jnp.ones((1, channels), jnp.float32)
    left = jnp.concatenate([-2.0 * v for v in sensors] + [s_high, s_low, 64.0 * one, one, 0.0 * one], 0)
    one = jnp.ones((1, points), jnp.float32)
    right = jnp.concatenate(places + [64.0 * one, one, g_high, g_low, 0.0 * one], 0)
    squares[...] = lax.dot_general(
        left.T.astype(jnp.bfloat16), right.astype(jnp.bfloat16), (((1,), (0,)), ((), ())),
        preferred_element_type=jnp.float32,
    )
    step = 32
    rates = [
        bins_ref[f + side * half].astype(jnp.float32) * (2.0 / samples) for f in range(half)
    ]

    @pl.loop(0, channels // step)
    def _(i):
        span = pl.ds(pl.multiple_of(i * step, step), step)
        square = squares[span, :]
        distance = square * lax.rsqrt(jnp.maximum(square, 1.0))
        for f in range(half):
            real, imag = scaled_cos_sin(distance * rates[f], channels ** (-0.5))
            beam_ref[f, 0, span, :] = real.astype(jnp.bfloat16)
            beam_ref[f, 1, span, :] = imag.astype(jnp.bfloat16)


def product_kernel(masks, first, last, *refs):
    blocks, rest = refs[: len(masks)], refs[len(masks) :]
    beams, rest = rest[:2], rest[2:]
    sums_in = None if first else rest[0]
    out = rest[-1]
    place = lax.axis_index("grid") // 2
    half = beams[0].shape[0]
    rows = blocks[0].shape[0] // half
    depth = blocks[0].shape[1]
    points = beams[0].shape[3]
    snaps = rows // 2
    for f in range(half):
        for b, beam in enumerate(beams):
            totals = [None, None]
            for part in range(2):
                total = None if first else sums_in[f, b, part]
                for mask, block in zip(masks, blocks):
                    start = pl.multiple_of((place ^ mask) * depth, depth)
                    term = jnp.dot(
                        block[pl.ds(f * rows, rows), :], beam[f, part, pl.ds(start, depth), :],
                        preferred_element_type=jnp.float32,
                    )
                    total = term if total is None else total + term
                totals[part] = total
            if last:
                real = totals[0][:snaps] + totals[1][snaps:]
                imag = totals[0][snaps:] - totals[1][:snaps]
                out[b, pl.ds(f, 1), :] = jnp.sum(real * real + imag * imag, 0, keepdims=True)
            else:
                for part in range(2):
                    out[f, b, part] = totals[part]


def vmem(n):
    return [pl.BlockSpec(memory_space=pltpu.VMEM)] * n


def grant(mib):
    return pltpu.CompilerParams(vmem_limit_bytes=mib << 20)


def near(*values):
    return [pltpu.with_memory_space_constraint(v, pltpu.VMEM) for v in values]


def on_device(series, bins, sensor_coords, grid_coords):
    snap_local, channel_local, samples = series.shape
    all_bins = bins.shape[0]
    channels = sensor_coords.shape[1]
    grid_local = grid_coords.shape[1]
    freq_size = lax.axis_size("freq")
    grid_size = lax.axis_size("grid")
    snap_total = snap_local * freq_size
    half = all_bins // 2
    rows = all_bins * snap_local
    side = lax.axis_index("grid") % 2

    def swap(value, axis, mask):
        size = lax.axis_size(axis)
        return lax.ppermute(value, axis, [(i, i ^ mask) for i in range(size)])

    packed = -(-3 * grid_local // channel_local // 16) * 16
    chunks = 4
    keep, send = pl.pallas_call(
        functools.partial(transform_kernel, half),
        out_shape=[
            pltpu.VMEM((rows, channel_local), jnp.bfloat16),
            pltpu.VMEM((rows + packed, channel_local), jnp.bfloat16),
        ],
        in_specs=[pl.BlockSpec(memory_space=pl.ANY)] * 3,
        out_specs=vmem(2),
        scratch_shapes=[
            pltpu.SMEM(bins.shape, jnp.int32),
            pltpu.VMEM(grid_coords.shape, jnp.int32),
            pltpu.VMEM(series.shape, jnp.bfloat16),
            pltpu.VMEM((snap_local * 2 * all_bins, channel_local), jnp.float32),
            pltpu.SemaphoreType.DMA((chunks,)),
            pltpu.SemaphoreType.DMA((2,)),
        ],
        compiler_params=grant(12),
    )(*[pltpu.with_memory_space_constraint(v, pltpu.HBM) for v in (bins, grid_coords, series)])
    received = swap(send, "grid", 1)

    def replicas(points, packed):
        return pl.pallas_call(
            functools.partial(replica_kernel, half, samples, packed),
            out_shape=pltpu.VMEM((half, 2, channels, grid_local), jnp.bfloat16),
            in_specs=[pl.BlockSpec(memory_space=pltpu.SMEM), *vmem(2)],
            out_specs=vmem(1)[0],
            scratch_shapes=[pltpu.VMEM((channels, grid_local), jnp.float32)],
            compiler_params=grant(12),
        )(bins, sensor_coords, points)

    pair = pl.pallas_call(
        pair_kernel,
        out_shape=pltpu.VMEM((rows, 2 * channel_local), jnp.bfloat16),
        in_specs=vmem(2),
        out_specs=vmem(1)[0],
        compiler_params=grant(12),
    )(*near(keep, received))
    far = {k: swap(pair, "grid", 2 * k) for k in range(1, grid_size // 2)}
    beams = (replicas(grid_coords, 0), replicas(*near(received), packed))
    sums = pl.pallas_call(
        functools.partial(product_kernel, (0,), True, False),
        out_shape=pltpu.VMEM((half, 2, 2, 2 * snap_local, grid_local), jnp.float32),
        in_specs=vmem(3),
        out_specs=vmem(1)[0],
        compiler_params=grant(12),
    )(*near(pair, *beams))
    masks = tuple(far)
    powers = pl.pallas_call(
        functools.partial(product_kernel, masks, False, True),
        out_shape=pltpu.VMEM((2, half, grid_local), jnp.float32),
        in_specs=vmem(len(masks) + 3),
        out_specs=vmem(1)[0],
        compiler_params=grant(12),
    )(*near(*[far[k] for k in masks], *beams, sums))
    total = jnp.concatenate([powers[0], swap(powers[1], "grid", 1)], 0)
    step = freq_size // 2
    while step:
        total = total + swap(total, "freq", step)
        step //= 2
    total = total / snap_total
    bin_count = all_bins // freq_size
    mine = (lax.axis_index("freq") * bin_count + side * half) % all_bins
    bin_power = lax.dynamic_slice_in_dim(total, mine, bin_count)
    power = jnp.sum(total, 0) / all_bins
    return (bin_power, power)


def solution(mesh):
    return jax.shard_map(
        on_device,
        mesh=mesh,
        in_specs=(P("freq", "grid", None), P(), P(), P(None, "grid")),
        out_specs=(P("freq", "grid"), P("grid")),
        check_vma=False,
    )
```

```python
import functools
import math

import jax
import jax.numpy as jnp
from jax import lax
from jax.experimental import pallas as pl
from jax.experimental.pallas import tpu as pltpu
from jax.sharding import PartitionSpec as P


def fit(function, degree):
    import numpy as np

    nodes = 0.125 + 0.125 * np.cos(math.pi * (np.arange(degree + 1) + 0.5) / (degree + 1))
    matrix = np.vander(nodes, degree + 1, increasing=True)
    return [float(v) for v in np.linalg.solve(matrix, function(np.sqrt(nodes)))]


def fits():
    import numpy as np

    return fit(lambda x: np.sin(math.pi * x) / x, 4), fit(lambda x: np.cos(math.pi * x), 4)


def horner(u, coefficients):
    total = coefficients[-1]
    for value in coefficients[-2::-1]:
        total = total * u + value
    return total


def scaled_cos_sin(turns, scale):
    whole = (turns + 12582912.0) - 12582912.0
    x = turns - whole
    u = x * x
    sine, cosine = fits()
    root = math.sqrt(2.0 * scale)
    s = x * horner(u, [v * root for v in sine])
    c = horner(u, [-v * root for v in cosine])
    return scale - s * s, s * c


def features(sensors_ref, places):
    channels, points = sensors_ref.shape[1], places[0].shape[1]
    sensors = [sensors_ref[pl.ds(a, 1), :].astype(jnp.float32) for a in range(3)]
    s_high, s_low = split(sum(v * v for v in sensors))
    g_high, g_low = split(sum(v * v for v in places))
    one = jnp.ones((1, channels), jnp.float32)
    left = jnp.concatenate([-2.0 * v for v in sensors] + [s_high, s_low, 64.0 * one, one, 0.0 * one], 0)
    one = jnp.ones((1, points), jnp.float32)
    right = jnp.concatenate(places + [64.0 * one, one, g_high, g_low, 0.0 * one], 0)
    return left.T.astype(jnp.bfloat16), right.astype(jnp.bfloat16)


def squared(left, right):
    return lax.dot_general(left, right, (((1,), (0,)), ((), ())), preferred_element_type=jnp.float32)


STEP = 32


def fill(beam_ref, squares, rates):
    scale = beam_ref.shape[2] ** (-0.5)

    @pl.loop(0, squares.shape[0] // STEP)
    def _(i):
        span = pl.ds(pl.multiple_of(i * STEP, STEP), STEP)
        square = squares[span, :]
        distance = square * lax.rsqrt(jnp.maximum(square, 1.0))
        for f, rate in rates.items():
            real, imag = scaled_cos_sin(distance * rate, scale)
            beam_ref[f, 0, span, :] = real.astype(jnp.bfloat16)
            beam_ref[f, 1, span, :] = imag.astype(jnp.bfloat16)


def rate_of(bins_ref, f, side, half, samples):
    return bins_ref[f + side * half].astype(jnp.float32) * (2.0 / samples)


def transform_kernel(
    half, bins_far, points_far, series_ref, keep_ref, send_ref, bins_ref, points_ref, held, tall, sems, small_sems,
):
    side = lax.axis_index("grid") % 2
    snaps, channels, samples = held.shape
    rows = tall.shape[0] // snaps
    all_bins = rows // 2
    chunks = sems.shape[0]
    step = snaps // chunks
    copies = [
        pltpu.make_async_copy(series_ref.at[pl.ds(i * step, step)], held.at[pl.ds(i * step, step)], sems.at[i])
        for i in range(chunks)
    ]
    small = [
        pltpu.make_async_copy(bins_far, bins_ref, small_sems.at[0]),
        pltpu.make_async_copy(points_far, points_ref, small_sems.at[1]),
    ]
    for copy in small:
        copy.start()
    for copy in copies:
        copy.start(priority=1)
    for copy in small:
        copy.wait()
    row = lax.broadcasted_iota(jnp.int32, (rows, samples), 0)
    sample = lax.broadcasted_iota(jnp.int32, (rows, samples), 1)
    number = jnp.zeros((rows, samples), jnp.int32)
    for f in range(all_bins):
        number = jnp.where(row // 2 == f, bins_ref[(f + side * half) % all_bins], number)
    turns = (number * sample).astype(jnp.float32) * (1.0 / samples)
    cosine, sine = scaled_cos_sin(turns, (samples / 2.0) ** (-0.5))
    table = jnp.where(row % 2 == 0, cosine, sine).astype(jnp.bfloat16)
    places = [points_ref[pl.ds(a, 1), :].astype(jnp.float32) for a in range(3)]
    extra = send_ref.shape[0] - rows // 2 * snaps
    pieces = [v[:, p : p + channels] for v in places for p in range(0, points_ref.shape[1], channels)]
    pieces.append(jnp.zeros((extra - len(pieces), channels), jnp.float32))
    send_ref[pl.ds(rows // 2 * snaps, extra), :] = jnp.concatenate(pieces, 0).astype(jnp.bfloat16)
    group = 2 if channels % 128 == 0 and step % 2 == 0 else 1
    for i, copy in enumerate(copies):
        copy.wait()
        for s in range(i * step, (i + 1) * step, group):
            block = held[s : s + group].reshape(group * channels, samples)
            out = lax.dot_general(table, block, (((1,), (1,)), ((), ())), preferred_element_type=jnp.float32)
            for p in range(group):
                tall[pl.ds((s + p) * rows, rows), :] = out[:, p * channels : (p + 1) * channels]
    for k in range(rows):
        picked = tall[pl.ds(k, snaps, stride=rows), :].astype(jnp.bfloat16)
        target, base = (keep_ref, k) if k < rows // 2 else (send_ref, k - rows // 2)
        target[pl.ds(base * snaps, snaps), :] = picked


def pair_kernel(keep_ref, received_ref, pair_ref):
    side = lax.axis_index("grid") % 2
    rows, channels = keep_ref.shape

    @pl.when(side == 0)
    def _():
        pair_ref[:, :channels] = keep_ref[...]
        pair_ref[:, channels:] = received_ref[:rows, :]

    @pl.when(side == 1)
    def _():
        pair_ref[:, channels:] = keep_ref[...]
        pair_ref[:, :channels] = received_ref[:rows, :]


def split(value):
    high = jnp.floor(value * (1.0 / 64.0))
    return high, value - 64.0 * high


def replica_kernel(half, samples, packed, bins_ref, sensors_ref, points_ref, beam_ref, squares):
    side = lax.axis_index("grid") % 2
    if packed:
        per = beam_ref.shape[3] // points_ref.shape[1]
        tail = points_ref[pl.ds(points_ref.shape[0] - packed, packed), :].astype(jnp.float32)
        places = [jnp.concatenate([tail[a * per + p : a * per + p + 1] for p in range(per)], 1) for a in range(3)]
    else:
        places = [points_ref[pl.ds(a, 1), :].astype(jnp.float32) for a in range(3)]
    squares[...] = squared(*features(sensors_ref, places))
    rates = {f: rate_of(bins_ref, f, side, half, samples) for f in range(half)}
    fill(beam_ref, squares, rates)


def product_kernel(masks, first, last, *refs):
    blocks, rest = refs[: len(masks)], refs[len(masks) :]
    beams, rest = rest[:2], rest[2:]
    sums_in = None if first else rest[0]
    out = rest[-1]
    place = lax.axis_index("grid") // 2
    half = beams[0].shape[0]
    rows = blocks[0].shape[0] // half
    depth = blocks[0].shape[1]
    points = beams[0].shape[3]
    snaps = rows // 2
    for f in range(half):
        for b, beam in enumerate(beams):
            totals = [None, None]
            for part in range(2):
                total = None if first else sums_in[f, b, part]
                for mask, block in zip(masks, blocks):
                    start = pl.multiple_of((place ^ mask) * depth, depth)
                    term = jnp.dot(
                        block[pl.ds(f * rows, rows), :], beam[f, part, pl.ds(start, depth), :],
                        preferred_element_type=jnp.float32,
                    )
                    total = term if total is None else total + term
                totals[part] = total
            if last:
                real = totals[0][:snaps] + totals[1][snaps:]
                imag = totals[0][snaps:] - totals[1][:snaps]
                out[b, pl.ds(f, 1), :] = jnp.sum(real * real + imag * imag, 0, keepdims=True)
            else:
                for part in range(2):
                    out[f, b, part] = totals[part]


def vmem(n):
    return [pl.BlockSpec(memory_space=pltpu.VMEM)] * n


def grant(mib):
    return pltpu.CompilerParams(vmem_limit_bytes=mib << 20)


def near(*values):
    return [pltpu.with_memory_space_constraint(v, pltpu.VMEM) for v in values]


def finish_kernel(snap_total, mine_ref, theirs_ref, bin_power_ref, power_ref, total_ref):
    bin_count = bin_power_ref.shape[0]
    half = mine_ref.shape[0] // 2
    first = (lax.axis_index("freq") * bin_count + lax.axis_index("grid") % 2 * half) % mine_ref.shape[0]
    total_ref[...] = (mine_ref[...] + theirs_ref[...]) / snap_total
    bin_power_ref[...] = total_ref[pl.ds(first, bin_count), :]
    power_ref[...] = jnp.sum(total_ref[...], 0, keepdims=True) / mine_ref.shape[0]


def on_device(series, bins, sensor_coords, grid_coords):
    snap_local, channel_local, samples = series.shape
    all_bins = bins.shape[0]
    channels = sensor_coords.shape[1]
    grid_local = grid_coords.shape[1]
    freq_size = lax.axis_size("freq")
    grid_size = lax.axis_size("grid")
    snap_total = snap_local * freq_size
    half = all_bins // 2
    rows = all_bins * snap_local

    def swap(value, mask):
        return lax.ppermute(value, "grid", [(i, i ^ mask) for i in range(grid_size)])

    packed = -(-3 * grid_local // channel_local // 16) * 16
    chunks = 2
    beam_type = pltpu.VMEM((half, 2, channels, grid_local), jnp.bfloat16)
    squares_type = pltpu.VMEM((channels, grid_local), jnp.float32)
    keep, send = pl.pallas_call(
        functools.partial(transform_kernel, half),
        out_shape=[
            pltpu.VMEM((rows, channel_local), jnp.bfloat16),
            pltpu.VMEM((rows + packed, channel_local), jnp.bfloat16),
        ],
        in_specs=[pl.BlockSpec(memory_space=pl.ANY)] * 3,
        out_specs=vmem(2),
        scratch_shapes=[
            pltpu.SMEM(bins.shape, jnp.int32),
            pltpu.VMEM(grid_coords.shape, jnp.int32),
            pltpu.VMEM(series.shape, jnp.bfloat16),
            pltpu.VMEM((snap_local * 2 * all_bins, channel_local), jnp.float32),
            pltpu.SemaphoreType.DMA((chunks,)),
            pltpu.SemaphoreType.DMA((2,)),
        ],
        compiler_params=grant(12),
    )(*[pltpu.with_memory_space_constraint(v, pltpu.HBM) for v in (bins, grid_coords, series)])
    received = swap(send, 1)

    def replicas(points, packed):
        return pl.pallas_call(
            functools.partial(replica_kernel, half, samples, packed),
            out_shape=beam_type,
            in_specs=[pl.BlockSpec(memory_space=pltpu.SMEM), *vmem(2)],
            out_specs=vmem(1)[0],
            scratch_shapes=[squares_type],
            compiler_params=grant(12),
        )(bins, sensor_coords, points)

    own_beam = replicas(grid_coords, 0)
    received, own_beam = lax.optimization_barrier((received, own_beam))
    pair = pl.pallas_call(
        pair_kernel,
        out_shape=pltpu.VMEM((rows, 2 * channel_local), jnp.bfloat16),
        in_specs=vmem(2),
        out_specs=vmem(1)[0],
        compiler_params=grant(12),
    )(*near(keep, received))
    far = {k: swap(pair, 2 * k) for k in range(1, grid_size // 2)}
    other_beam = replicas(*near(received), packed)
    beams = (own_beam, other_beam)
    sums = pl.pallas_call(
        functools.partial(product_kernel, (0,), True, False),
        out_shape=pltpu.VMEM((half, 2, 2, 2 * snap_local, grid_local), jnp.float32),
        in_specs=vmem(3),
        out_specs=vmem(1)[0],
        compiler_params=grant(12),
    )(*near(pair, *beams))
    masks = tuple(far)
    powers = pl.pallas_call(
        functools.partial(product_kernel, masks, False, True),
        out_shape=pltpu.VMEM((2, half, grid_local), jnp.float32),
        in_specs=vmem(len(masks) + 3),
        out_specs=vmem(1)[0],
        compiler_params=grant(12),
    )(*near(*[far[k] for k in masks], *beams, sums))
    def across(value, freq_mask, grid_mask):
        every = [(f, g) for f in range(freq_size) for g in range(grid_size)]
        index = lambda f, g: f * grid_size + g
        pairs = [(index(f, g), index(f ^ freq_mask, g ^ grid_mask)) for f, g in every]
        return lax.ppermute(value, ("freq", "grid"), pairs)

    mine, theirs = powers[0], powers[1]
    masks = list(range(2, freq_size, 2))
    apart = [across(theirs, m, 1) for m in masks]
    beside = [across(mine, m, 0) for m in masks]
    crossed = across(theirs, 0, 1)
    total = jnp.concatenate([sum(beside, mine), sum(apart, crossed)], 0)
    returned = across(total, 1, 0)
    bin_power, power = pl.pallas_call(
        functools.partial(finish_kernel, snap_total),
        out_shape=[
            jax.ShapeDtypeStruct((all_bins // freq_size, grid_local), jnp.float32),
            jax.ShapeDtypeStruct((1, grid_local), jnp.float32),
        ],
        in_specs=vmem(2),
        out_specs=vmem(2),
        scratch_shapes=[pltpu.VMEM((all_bins, grid_local), jnp.float32)],
        compiler_params=grant(12),
    )(*near(total, returned))
    return (bin_power, power.reshape(grid_local))


def solution(mesh):
    return jax.shard_map(
        on_device,
        mesh=mesh,
        in_specs=(P("freq", "grid", None), P(), P(), P(None, "grid")),
        out_specs=(P("freq", "grid"), P("grid")),
        check_vma=False,
    )
```

```python
import functools
import math

import jax
import jax.numpy as jnp
from jax import lax
from jax.experimental import pallas as pl
from jax.experimental.pallas import tpu as pltpu
from jax.sharding import PartitionSpec as P


def fit(function, degree):
    import numpy as np

    nodes = 0.125 + 0.125 * np.cos(math.pi * (np.arange(degree + 1) + 0.5) / (degree + 1))
    matrix = np.vander(nodes, degree + 1, increasing=True)
    return [float(v) for v in np.linalg.solve(matrix, function(np.sqrt(nodes)))]


def fits():
    import numpy as np

    return fit(lambda x: np.sin(math.pi * x) / x, 4), fit(lambda x: np.cos(math.pi * x), 4)


def horner(u, coefficients):
    total = coefficients[-1]
    for value in coefficients[-2::-1]:
        total = total * u + value
    return total


def scaled_cos_sin(turns, scale):
    whole = (turns + 12582912.0) - 12582912.0
    x = turns - whole
    u = x * x
    sine, cosine = fits()
    root = math.sqrt(2.0 * scale)
    s = x * horner(u, [v * root for v in sine])
    c = horner(u, [-v * root for v in cosine])
    return scale - s * s, s * c


def features(sensors_ref, places):
    channels, points = sensors_ref.shape[1], places[0].shape[1]
    sensors = [sensors_ref[pl.ds(a, 1), :].astype(jnp.float32) for a in range(3)]
    s_high, s_low = split(sum(v * v for v in sensors))
    g_high, g_low = split(sum(v * v for v in places))
    one = jnp.ones((1, channels), jnp.float32)
    left = jnp.concatenate([-2.0 * v for v in sensors] + [s_high, s_low, 64.0 * one, one, 0.0 * one], 0)
    one = jnp.ones((1, points), jnp.float32)
    right = jnp.concatenate(places + [64.0 * one, one, g_high, g_low, 0.0 * one], 0)
    return left.T.astype(jnp.bfloat16), right.astype(jnp.bfloat16)


def squared(left, right):
    return lax.dot_general(left, right, (((1,), (0,)), ((), ())), preferred_element_type=jnp.float32)


STEP = 32


def fill(beam_ref, squares, rates):
    scale = beam_ref.shape[2] ** (-0.5)

    @pl.loop(0, squares.shape[0] // STEP)
    def _(i):
        span = pl.ds(pl.multiple_of(i * STEP, STEP), STEP)
        square = squares[span, :]
        distance = square * lax.rsqrt(jnp.maximum(square, 1.0))
        for f in range(beam_ref.shape[0]):
            real, imag = scaled_cos_sin(distance * rates[f], scale)
            beam_ref[f, 0, span, :] = real.astype(jnp.bfloat16)
            beam_ref[f, 1, span, :] = imag.astype(jnp.bfloat16)


def bin_at(bins_ref, f):
    return bins_ref[:, f : f + 1].astype(jnp.float32)


def transform_kernel(bins_far, series_ref, spectra_ref, bins_ref, held, tall, sems, small_sem):
    snaps, channels, samples = held.shape
    rows = tall.shape[0] // snaps
    all_bins = rows // 2
    chunks = sems.shape[0]
    step = snaps // chunks
    copies = [
        pltpu.make_async_copy(series_ref.at[pl.ds(i * step, step)], held.at[pl.ds(i * step, step)], sems.at[i])
        for i in range(chunks)
    ]
    small = pltpu.make_async_copy(bins_far, bins_ref, small_sem)
    small.start()
    for copy in copies:
        copy.start(priority=1)
    small.wait()
    row = lax.broadcasted_iota(jnp.int32, (rows, samples), 0)
    sample = lax.broadcasted_iota(jnp.int32, (rows, samples), 1)
    number = jnp.zeros((rows, samples), jnp.float32)
    for f in range(all_bins):
        number = jnp.where(row // 2 == f, bin_at(bins_ref, f), number)
    turns = number * sample.astype(jnp.float32) * (1.0 / samples)
    cosine, sine = scaled_cos_sin(turns, (samples / 2.0) ** (-0.5))
    table = jnp.where(row % 2 == 0, cosine, sine).astype(jnp.bfloat16)
    group = 2 if channels % 128 == 0 and step % 2 == 0 else 1
    for i, copy in enumerate(copies):
        copy.wait()
        for s in range(i * step, (i + 1) * step, group):
            block = held[s : s + group].reshape(group * channels, samples)
            out = lax.dot_general(table, block, (((1,), (1,)), ((), ())), preferred_element_type=jnp.float32)
            for p in range(group):
                tall[pl.ds((s + p) * rows, rows), :] = out[:, p * channels : (p + 1) * channels]
    for k in range(rows):
        picked = tall[pl.ds(k, snaps, stride=rows), :].astype(jnp.bfloat16)
        spectra_ref[pl.ds(k * snaps, snaps), :] = picked


def stack_kernel(*refs):
    out = refs[-1]
    for k, ref in enumerate(refs[:-1]):
        out[pl.ds(k * ref.shape[0], ref.shape[0]), :] = ref[...]


def split(value):
    high = jnp.floor(value * (1.0 / 64.0))
    return high, value - 64.0 * high


def replica_kernel(bins, samples, first, bins_ref, sensors_ref, points_ref, *refs):
    if first:
        beam_ref, squares, rates = refs
        places = [points_ref[pl.ds(a, 1), :].astype(jnp.float32) for a in range(3)]
        squares[...] = squared(*features(sensors_ref, places))
    else:
        squares, beam_ref, rates = refs
    for i, f in enumerate(bins):
        rates[i] = jnp.broadcast_to(bin_at(bins_ref, f) * (2.0 / samples), rates.shape[1:])
    fill(beam_ref, squares, rates)


def product_kernel(masks, last, *refs):
    blocks, beams, rest = refs[: len(masks)], refs[len(masks) : len(masks) + 2], refs[len(masks) + 2 :]
    out = rest[-1]
    sums = rest[0] if last else out
    place = lax.axis_index("grid")
    half = beams[0].shape[0]
    depth = blocks[0].shape[1]
    rows = sums.shape[2]
    snaps = rows // 2
    for f in range(2 * half):
        beam = beams[f // half]
        totals = []
        for part in range(2):
            total = rest[0][f, part] if last else None
            for block, inside in zip(blocks, masks):
                for i, mask in enumerate(inside):
                    start = pl.multiple_of((place ^ mask) * depth, depth)
                    term = jnp.dot(
                        block[pl.ds((i * 2 * half + f) * rows, rows), :], beam[f % half, part, pl.ds(start, depth), :],
                        preferred_element_type=jnp.float32,
                    )
                    total = term if total is None else total + term
            totals.append(total)
        if last:
            real = totals[0][:snaps] + totals[1][snaps:]
            imag = totals[0][snaps:] - totals[1][:snaps]
            out[pl.ds(f, 1), :] = jnp.sum(real * real + imag * imag, 0, keepdims=True)
        else:
            for part in range(2):
                out[f, part] = totals[part]


def vmem(n):
    return [pl.BlockSpec(memory_space=pltpu.VMEM)] * n


def grant(mib):
    return pltpu.CompilerParams(vmem_limit_bytes=mib << 20)


def near(*values):
    return [pltpu.with_memory_space_constraint(v, pltpu.VMEM) for v in values]


def finish_kernel(snap_total, mine_ref, theirs_ref, bin_power_ref, power_ref, total_ref):
    bin_count = bin_power_ref.shape[0]
    total_ref[...] = (mine_ref[...] + theirs_ref[...]) / snap_total
    bin_power_ref[...] = total_ref[pl.ds(lax.axis_index("freq") * bin_count, bin_count), :]
    power_ref[...] = jnp.sum(total_ref[...], 0, keepdims=True) / mine_ref.shape[0]


def on_device(series, bins, sensor_coords, grid_coords):
    snap_local, channel_local, samples = series.shape
    all_bins = bins.shape[0]
    channels = sensor_coords.shape[1]
    grid_local = grid_coords.shape[1]
    freq_size = lax.axis_size("freq")
    grid_size = lax.axis_size("grid")
    snap_total = snap_local * freq_size
    half = all_bins // 2
    rows = 2 * all_bins * snap_local

    def swap(value, axis, mask):
        size = lax.axis_size(axis)
        return lax.ppermute(value, axis, [(i, i ^ mask) for i in range(size)])

    def call(kernel, out_shape, inputs, scratch=(), near_inputs=True):
        outs = out_shape if isinstance(out_shape, list) else [out_shape]
        result = pl.pallas_call(
            kernel,
            out_shape=outs,
            in_specs=vmem(len(inputs)) if near_inputs else [pl.BlockSpec(memory_space=pl.ANY)] * len(inputs),
            out_specs=vmem(len(outs)),
            scratch_shapes=scratch,
            compiler_params=grant(12),
        )(*inputs)
        return result if isinstance(out_shape, list) else result[0]

    chunks = 2
    bins_row = bins.reshape(1, all_bins)
    spectra = call(
        transform_kernel,
        pltpu.VMEM((rows, channel_local), jnp.bfloat16),
        [pltpu.with_memory_space_constraint(v, pltpu.HBM) for v in (bins_row, series)],
        [
            pltpu.VMEM((1, all_bins), jnp.int32),
            pltpu.VMEM(series.shape, jnp.bfloat16),
            pltpu.VMEM((rows, channel_local), jnp.float32),
            pltpu.SemaphoreType.DMA((chunks,)),
            pltpu.SemaphoreType.DMA,
        ],
        near_inputs=False,
    )
    far = []
    for k in range(1, grid_size // 2):
        far.append(swap(spectra, "grid", 2 * k))
    near_spectra = swap(spectra, "grid", 1)
    beam_type = pltpu.VMEM((half, 2, channels, grid_local), jnp.bfloat16)
    squares_type = pltpu.VMEM((channels, grid_local), jnp.float32)
    rates_type = pltpu.VMEM((half, STEP, grid_local), jnp.float32)
    beam0, squares = call(
        functools.partial(replica_kernel, range(half), samples, True),
        [beam_type, squares_type], [bins_row, sensor_coords, grid_coords], [rates_type],
    )
    stacked = call(stack_kernel, pltpu.VMEM((len(far) * rows, channel_local), jnp.bfloat16), near(*far))
    rest = swap(stacked, "grid", 1)
    beam1 = call(
        functools.partial(replica_kernel, range(half, all_bins), samples, False),
        beam_type, [bins_row, sensor_coords, grid_coords, *near(squares)], [rates_type],
    )
    masks = [2 * k for k in range(1, grid_size // 2)]
    sums = call(
        functools.partial(product_kernel, [[0], *[[m] for m in masks], [1]], False),
        pltpu.VMEM((all_bins, 2, 2 * snap_local, grid_local), jnp.float32),
        near(spectra, *far, near_spectra, beam0, beam1),
    )
    total = call(
        functools.partial(product_kernel, [[m + 1 for m in masks]], True),
        pltpu.VMEM((all_bins, grid_local), jnp.float32),
        near(rest, beam0, beam1, sums),
    )
    step = freq_size // 2
    while step > 1:
        total += swap(total, "freq", step)
        step //= 2
    bin_power, power = call(
        functools.partial(finish_kernel, snap_total),
        [
            jax.ShapeDtypeStruct((all_bins // freq_size, grid_local), jnp.float32),
            jax.ShapeDtypeStruct((1, grid_local), jnp.float32),
        ],
        near(total, swap(total, "freq", 1)),
        [pltpu.VMEM((all_bins, grid_local), jnp.float32)],
    )
    return (bin_power, power.reshape(grid_local))


def solution(mesh):
    return jax.shard_map(
        on_device,
        mesh=mesh,
        in_specs=(P("freq", "grid", None), P(), P(), P(None, "grid")),
        out_specs=(P("freq", "grid"), P("grid")),
        check_vma=False,
    )
```

```python
import functools
import math

import jax
import jax.numpy as jnp
from jax import lax
from jax.experimental import pallas as pl
from jax.experimental.pallas import tpu as pltpu
from jax.sharding import PartitionSpec as P


def fit(function, degree):
    import numpy as np

    nodes = 0.125 + 0.125 * np.cos(math.pi * (np.arange(degree + 1) + 0.5) / (degree + 1))
    matrix = np.vander(nodes, degree + 1, increasing=True)
    return [float(v) for v in np.linalg.solve(matrix, function(np.sqrt(nodes)))]


def fits():
    import numpy as np

    return fit(lambda x: np.sin(math.pi * x) / x, 4), fit(lambda x: np.cos(math.pi * x), 4)


def horner(u, coefficients):
    total = coefficients[-1]
    for value in coefficients[-2::-1]:
        total = total * u + value
    return total


def scaled_cos_sin(turns, scale):
    whole = (turns + 12582912.0) - 12582912.0
    x = turns - whole
    u = x * x
    sine, cosine = fits()
    root = math.sqrt(2.0 * scale)
    s = x * horner(u, [v * root for v in sine])
    c = horner(u, [-v * root for v in cosine])
    return scale - s * s, s * c


def features(sensors_ref, places):
    channels, points = sensors_ref.shape[1], places[0].shape[1]
    sensors = [sensors_ref[pl.ds(a, 1), :].astype(jnp.float32) for a in range(3)]
    s_high, s_low = split(sum(v * v for v in sensors))
    g_high, g_low = split(sum(v * v for v in places))
    one = jnp.ones((1, channels), jnp.float32)
    left = jnp.concatenate([-2.0 * v for v in sensors] + [s_high, s_low, 64.0 * one, one, 0.0 * one], 0)
    one = jnp.ones((1, points), jnp.float32)
    right = jnp.concatenate(places + [64.0 * one, one, g_high, g_low, 0.0 * one], 0)
    return left.T.astype(jnp.bfloat16), right.astype(jnp.bfloat16)


def squared(left, right):
    return lax.dot_general(left, right, (((1,), (0,)), ((), ())), preferred_element_type=jnp.float32)


STEP = 32


def fill(beam_ref, squares, rates):
    scale = beam_ref.shape[2] ** (-0.5)

    @pl.loop(0, squares.shape[0] // STEP)
    def _(i):
        span = pl.ds(pl.multiple_of(i * STEP, STEP), STEP)
        square = squares[span, :]
        distance = square * lax.rsqrt(jnp.maximum(square, 1.0))
        for f in range(beam_ref.shape[0]):
            real, imag = scaled_cos_sin(distance * rates[f], scale)
            beam_ref[f, 0, span, :] = real.astype(jnp.bfloat16)
            beam_ref[f, 1, span, :] = imag.astype(jnp.bfloat16)


def bin_at(bins_ref, f):
    return bins_ref[:, f : f + 1].astype(jnp.float32)


def transform_kernel(bins_far, series_ref, spectra_ref, bins_ref, held, tall, sems, small_sem):
    snaps, channels, samples = held.shape
    rows = tall.shape[0] // snaps
    all_bins = rows // 2
    chunks = sems.shape[0]
    step = snaps // chunks
    copies = [
        pltpu.make_async_copy(series_ref.at[pl.ds(i * step, step)], held.at[pl.ds(i * step, step)], sems.at[i])
        for i in range(chunks)
    ]
    small = pltpu.make_async_copy(bins_far, bins_ref, small_sem)
    small.start()
    for copy in copies:
        copy.start(priority=1)
    small.wait()
    row = lax.broadcasted_iota(jnp.int32, (rows, samples), 0)
    sample = lax.broadcasted_iota(jnp.int32, (rows, samples), 1)
    number = jnp.zeros((rows, samples), jnp.float32)
    for f in range(all_bins):
        number = jnp.where(row // 2 == f, bin_at(bins_ref, f), number)
    turns = number * sample.astype(jnp.float32) * (1.0 / samples)
    cosine, sine = scaled_cos_sin(turns, (samples / 2.0) ** (-0.5))
    table = jnp.where(row % 2 == 0, cosine, sine).astype(jnp.bfloat16)
    group = 2 if channels % 128 == 0 and step % 2 == 0 else 1
    for i, copy in enumerate(copies):
        copy.wait()
        for s in range(i * step, (i + 1) * step, group):
            block = held[s : s + group].reshape(group * channels, samples)
            out = lax.dot_general(table, block, (((1,), (1,)), ((), ())), preferred_element_type=jnp.float32)
            for p in range(group):
                tall[pl.ds((s + p) * rows, rows), :] = out[:, p * channels : (p + 1) * channels]
    for k in range(rows):
        picked = tall[pl.ds(k, snaps, stride=rows), :].astype(jnp.bfloat16)
        spectra_ref[pl.ds(k * snaps, snaps), :] = picked


def stack_kernel(*refs):
    out = refs[-1]
    for k, ref in enumerate(refs[:-1]):
        out[pl.ds(k * ref.shape[0], ref.shape[0]), :] = ref[...]


def split(value):
    high = jnp.floor(value * (1.0 / 64.0))
    return high, value - 64.0 * high


def replica_kernel(bins, samples, first, bins_ref, sensors_ref, points_ref, *refs):
    if first:
        beam_ref, squares, rates = refs
        places = [points_ref[pl.ds(a, 1), :].astype(jnp.float32) for a in range(3)]
        squares[...] = squared(*features(sensors_ref, places))
    else:
        squares, beam_ref, rates = refs
    for i, f in enumerate(bins):
        rates[i] = jnp.broadcast_to(bin_at(bins_ref, f) * (2.0 / samples), rates.shape[1:])
    fill(beam_ref, squares, rates)


def product_kernel(masks, last, *refs):
    blocks, beams, rest = refs[: len(masks)], refs[len(masks) : len(masks) + 2], refs[len(masks) + 2 :]
    out = rest[-1]
    sums = rest[0] if last else out
    place = lax.axis_index("grid")
    half = beams[0].shape[0]
    depth = blocks[0].shape[1]
    rows = sums.shape[2]
    snaps = rows // 2
    for f in range(2 * half):
        beam = beams[f // half]
        totals = []
        for part in range(2):
            total = rest[0][f, part] if last else None
            for block, inside in zip(blocks, masks):
                for i, mask in enumerate(inside):
                    start = pl.multiple_of((place ^ mask) * depth, depth)
                    term = jnp.dot(
                        block[pl.ds((i * 2 * half + f) * rows, rows), :], beam[f % half, part, pl.ds(start, depth), :],
                        preferred_element_type=jnp.float32,
                    )
                    total = term if total is None else total + term
            totals.append(total)
        if last:
            real = totals[0][:snaps] + totals[1][snaps:]
            imag = totals[0][snaps:] - totals[1][:snaps]
            out[pl.ds(f, 1), :] = jnp.sum(real * real + imag * imag, 0, keepdims=True)
        else:
            for part in range(2):
                out[f, part] = totals[part]


def vmem(n):
    return [pl.BlockSpec(memory_space=pltpu.VMEM)] * n


def grant(mib):
    return pltpu.CompilerParams(vmem_limit_bytes=mib << 20)


def near(*values):
    return [pltpu.with_memory_space_constraint(v, pltpu.VMEM) for v in values]


def finish_kernel(snap_total, mine_ref, second_ref, third_ref, fourth_ref, bin_power_ref, power_ref, total_ref):
    bin_count = bin_power_ref.shape[0]
    total_ref[...] = ((mine_ref[...] + second_ref[...]) + (third_ref[...] + fourth_ref[...])) / snap_total
    bin_power_ref[...] = total_ref[pl.ds(lax.axis_index("freq") * bin_count, bin_count), :]
    power_ref[...] = jnp.sum(total_ref[...], 0, keepdims=True) / mine_ref.shape[0]


def on_device(series, bins, sensor_coords, grid_coords):
    snap_local, channel_local, samples = series.shape
    all_bins = bins.shape[0]
    channels = sensor_coords.shape[1]
    grid_local = grid_coords.shape[1]
    freq_size = lax.axis_size("freq")
    grid_size = lax.axis_size("grid")
    snap_total = snap_local * freq_size
    half = all_bins // 2
    rows = 2 * all_bins * snap_local

    def swap(value, axis, mask):
        size = lax.axis_size(axis)
        return lax.ppermute(value, axis, [(i, i ^ mask) for i in range(size)])

    def call(kernel, out_shape, inputs, scratch=(), near_inputs=True):
        outs = out_shape if isinstance(out_shape, list) else [out_shape]
        result = pl.pallas_call(
            kernel,
            out_shape=outs,
            in_specs=vmem(len(inputs)) if near_inputs else [pl.BlockSpec(memory_space=pl.ANY)] * len(inputs),
            out_specs=vmem(len(outs)),
            scratch_shapes=scratch,
            compiler_params=grant(12),
        )(*inputs)
        return result if isinstance(out_shape, list) else result[0]

    chunks = 2
    bins_row = bins.reshape(1, all_bins)
    spectra = call(
        transform_kernel,
        pltpu.VMEM((rows, channel_local), jnp.bfloat16),
        [pltpu.with_memory_space_constraint(v, pltpu.HBM) for v in (bins_row, series)],
        [
            pltpu.VMEM((1, all_bins), jnp.int32),
            pltpu.VMEM(series.shape, jnp.bfloat16),
            pltpu.VMEM((rows, channel_local), jnp.float32),
            pltpu.SemaphoreType.DMA((chunks,)),
            pltpu.SemaphoreType.DMA,
        ],
        near_inputs=False,
    )
    far = {}
    for k in range(1, grid_size // 2):
        far[k] = swap(spectra, "grid", 2 * k)

    def stack(*values):
        return call(stack_kernel, pltpu.VMEM((len(values) * rows, channel_local), jnp.bfloat16), near(*values))

    near_spectra = swap(spectra, "grid", 1)
    beam_type = pltpu.VMEM((half, 2, channels, grid_local), jnp.bfloat16)
    squares_type = pltpu.VMEM((channels, grid_local), jnp.float32)
    rates_type = pltpu.VMEM((half, STEP, grid_local), jnp.float32)
    beam0, squares = call(
        functools.partial(replica_kernel, range(half), samples, True),
        [beam_type, squares_type], [bins_row, sensor_coords, grid_coords], [rates_type],
    )
    rest = swap(stack(*far.values()), "grid", 1)
    beam1 = call(
        functools.partial(replica_kernel, range(half, all_bins), samples, False),
        beam_type, [bins_row, sensor_coords, grid_coords, *near(squares)], [rates_type],
    )
    sums = call(
        functools.partial(product_kernel, [[0], *[[2 * k] for k in far], [1]], False),
        pltpu.VMEM((all_bins, 2, 2 * snap_local, grid_local), jnp.float32),
        near(spectra, *far.values(), near_spectra, beam0, beam1),
    )
    total = call(
        functools.partial(product_kernel, [[2 * k + 1 for k in far]], True),
        pltpu.VMEM((all_bins, grid_local), jnp.float32),
        near(rest, beam0, beam1, sums),
    )
    step = freq_size // 2
    while step > 2:
        total += swap(total, "freq", step)
        step //= 2
    others = []
    for mask in (2, 3, 1):
        others.append(swap(total, "freq", mask))
    bin_power, power = call(
        functools.partial(finish_kernel, snap_total),
        [
            jax.ShapeDtypeStruct((all_bins // freq_size, grid_local), jnp.float32),
            jax.ShapeDtypeStruct((1, grid_local), jnp.float32),
        ],
        near(total, *others),
        [pltpu.VMEM((all_bins, grid_local), jnp.float32)],
    )
    return (bin_power, power.reshape(grid_local))


def solution(mesh):
    return jax.shard_map(
        on_device,
        mesh=mesh,
        in_specs=(P("freq", "grid", None), P(), P(), P(None, "grid")),
        out_specs=(P("freq", "grid"), P("grid")),
        check_vma=False,
    )
```

```python
import functools
import math

import jax
import jax.numpy as jnp
from jax import lax
from jax.experimental import pallas as pl
from jax.experimental.pallas import tpu as pltpu
from jax.sharding import PartitionSpec as P


def fit(function, degree):
    import numpy as np

    nodes = 0.125 + 0.125 * np.cos(math.pi * (np.arange(degree + 1) + 0.5) / (degree + 1))
    matrix = np.vander(nodes, degree + 1, increasing=True)
    return [float(v) for v in np.linalg.solve(matrix, function(np.sqrt(nodes)))]


def half_sine():
    import numpy as np

    return fit(lambda x: np.sin(math.pi * x) / x, 4)


def horner(u, coefficients):
    total = coefficients[-1]
    for value in coefficients[-2::-1]:
        total = total * u + value
    return total


def scaled_cos_sin(turns, scale):
    whole = (turns + 12582912.0) - 12582912.0
    x = turns - whole
    root = math.sqrt(2.0 * scale)
    s = x * horner(x * x, [-v * root for v in half_sine()])
    real = scale - s * s
    rest = jnp.maximum(real + scale, 1e-30)
    return real, s * (rest * lax.rsqrt(rest))


def features(sensors_ref, places):
    channels, points = sensors_ref.shape[1], places[0].shape[1]
    sensors = [sensors_ref[pl.ds(a, 1), :].astype(jnp.float32) for a in range(3)]
    s_high, s_low = split(sum(v * v for v in sensors))
    g_high, g_low = split(sum(v * v for v in places))
    one = jnp.ones((1, channels), jnp.float32)
    left = jnp.concatenate([-2.0 * v for v in sensors] + [s_high, s_low, 64.0 * one, one, 0.0 * one], 0)
    one = jnp.ones((1, points), jnp.float32)
    right = jnp.concatenate(places + [64.0 * one, one, g_high, g_low, 0.0 * one], 0)
    return left.T.astype(jnp.bfloat16), right.astype(jnp.bfloat16)


def squared(left, right):
    return lax.dot_general(left, right, (((1,), (0,)), ((), ())), preferred_element_type=jnp.float32)


STEP = 64
TOGETHER = 1


def fill(beam_ref, squares, rates):
    channels = squares.shape[0]
    scale = channels ** (-0.5)
    together = TOGETHER if channels % (STEP * TOGETHER) == 0 else 1

    @pl.loop(0, channels // (STEP * together))
    def _(i):
        for part in range(together):
            span = pl.ds(pl.multiple_of((i * together + part) * STEP, STEP), STEP)
            square = squares[span, :]
            distance = square * lax.rsqrt(jnp.maximum(square, 1.0))
            for f in range(beam_ref.shape[0]):
                real, imag = scaled_cos_sin(distance * rates[f], scale)
                beam_ref[f, 0, span, :] = real.astype(jnp.bfloat16)
                beam_ref[f, 1, span, :] = imag.astype(jnp.bfloat16)


def bin_at(bins_ref, f):
    return bins_ref[:, f : f + 1].astype(jnp.float32)


def transform_kernel(
    bins_far, sensors_far, points_far, series_ref, spectra_ref, bins_ref, sensors_ref, points_ref, held, tall, sems, small_sems
):
    snaps, channels, samples = held.shape
    rows = tall.shape[0] // snaps
    all_bins = rows // 2
    chunks = sems.shape[0]
    step = snaps // chunks
    copies = [
        pltpu.make_async_copy(series_ref.at[pl.ds(i * step, step)], held.at[pl.ds(i * step, step)], sems.at[i])
        for i in range(chunks)
    ]
    small = [
        pltpu.make_async_copy(a, b, small_sems.at[i])
        for i, (a, b) in enumerate([(bins_far, bins_ref), (sensors_far, sensors_ref), (points_far, points_ref)])
    ]
    small[0].start()
    for copy in copies:
        copy.start(priority=1)
    for copy in small[1:]:
        copy.start()
    small[0].wait()
    row = lax.broadcasted_iota(jnp.int32, (rows, samples), 0)
    sample = lax.broadcasted_iota(jnp.int32, (rows, samples), 1)
    number = jnp.zeros((rows, samples), jnp.float32)
    for f in range(all_bins):
        number = jnp.where(row // 2 == f, bin_at(bins_ref, f), number)
    turns = number * sample.astype(jnp.float32) * (1.0 / samples)
    cosine, sine = scaled_cos_sin(turns, (samples / 2.0) ** (-0.5))
    table = jnp.where(row % 2 == 0, cosine, sine).astype(jnp.bfloat16)
    group = 2 if channels % 128 == 0 and step % 2 == 0 else 1
    for i, copy in enumerate(copies):
        copy.wait()
        for s in range(i * step, (i + 1) * step, group):
            block = held[s : s + group].reshape(group * channels, samples)
            out = lax.dot_general(table, block, (((1,), (1,)), ((), ())), preferred_element_type=jnp.float32)
            for p in range(group):
                tall[pl.ds((s + p) * rows, rows), :] = out[:, p * channels : (p + 1) * channels]
    for copy in small[1:]:
        copy.wait()
    for k in range(rows):
        picked = tall[pl.ds(k, snaps, stride=rows), :].astype(jnp.bfloat16)
        spectra_ref[pl.ds(k * snaps, snaps), :] = picked


def stack_kernel(*refs):
    out = refs[-1]
    for k, ref in enumerate(refs[:-1]):
        out[pl.ds(k * ref.shape[0], ref.shape[0]), :] = ref[...]


def split(value):
    high = jnp.floor(value * (1.0 / 64.0))
    return high, value - 64.0 * high


def replica_kernel(bins, samples, first, bins_ref, sensors_ref, points_ref, *refs):
    if first:
        beam_ref, squares, rates = refs
        places = [points_ref[pl.ds(a, 1), :].astype(jnp.float32) for a in range(3)]
        squares[...] = squared(*features(sensors_ref, places))
    else:
        squares, beam_ref, rates = refs
    for i, f in enumerate(bins):
        rates[i] = jnp.broadcast_to(bin_at(bins_ref, f) * (2.0 / samples), rates.shape[1:])
    fill(beam_ref, squares, rates)


def product_kernel(masks, last, *refs):
    blocks, beams, rest = refs[: len(masks)], refs[len(masks) : len(masks) + 2], refs[len(masks) + 2 :]
    out = rest[-1]
    sums = rest[0] if last else out
    place = lax.axis_index("grid")
    counts = [beam.shape[0] for beam in beams]
    bins = sum(counts)
    depth = blocks[0].shape[1]
    rows = sums.shape[2]
    snaps = rows // 2
    for f in range(bins):
        beam, at = (beams[0], f) if f < counts[0] else (beams[1], f - counts[0])
        totals = []
        for part in range(2):
            total = rest[0][f, part] if last else None
            for block, inside in zip(blocks, masks):
                for i, mask in enumerate(inside):
                    start = pl.multiple_of((place ^ mask) * depth, depth)
                    term = jnp.dot(
                        block[pl.ds((i * bins + f) * rows, rows), :], beam[at, part, pl.ds(start, depth), :],
                        preferred_element_type=jnp.float32,
                    )
                    total = term if total is None else total + term
            totals.append(total)
        if last:
            real = totals[0][:snaps] + totals[1][snaps:]
            imag = totals[0][snaps:] - totals[1][:snaps]
            out[pl.ds(f, 1), :] = jnp.sum(real * real + imag * imag, 0, keepdims=True)
        else:
            for part in range(2):
                out[f, part] = totals[part]


def vmem(n):
    return [pl.BlockSpec(memory_space=pltpu.VMEM)] * n


def grant(mib):
    return pltpu.CompilerParams(vmem_limit_bytes=mib << 20)


def near(*values):
    return [pltpu.with_memory_space_constraint(v, pltpu.VMEM) for v in values]


def finish_kernel(snap_total, mine_ref, second_ref, third_ref, fourth_ref, bin_power_ref, power_ref, total_ref):
    bin_count = bin_power_ref.shape[0]
    total_ref[...] = ((mine_ref[...] + second_ref[...]) + (third_ref[...] + fourth_ref[...])) / snap_total
    bin_power_ref[...] = total_ref[pl.ds(lax.axis_index("freq") * bin_count, bin_count), :]
    power_ref[...] = jnp.sum(total_ref[...], 0, keepdims=True) / mine_ref.shape[0]


def on_device(series, bins, sensor_coords, grid_coords):
    snap_local, channel_local, samples = series.shape
    all_bins = bins.shape[0]
    channels = sensor_coords.shape[1]
    grid_local = grid_coords.shape[1]
    freq_size = lax.axis_size("freq")
    grid_size = lax.axis_size("grid")
    snap_total = snap_local * freq_size
    half = all_bins // 2
    rows = 2 * all_bins * snap_local

    def swap(value, axis, mask):
        size = lax.axis_size(axis)
        return lax.ppermute(value, axis, [(i, i ^ mask) for i in range(size)])

    def call(kernel, out_shape, inputs, scratch=(), near_inputs=True):
        outs = out_shape if isinstance(out_shape, list) else [out_shape]
        result = pl.pallas_call(
            kernel,
            out_shape=outs,
            in_specs=vmem(len(inputs)) if near_inputs else [pl.BlockSpec(memory_space=pl.ANY)] * len(inputs),
            out_specs=vmem(len(outs)),
            scratch_shapes=scratch,
            compiler_params=grant(12),
        )(*inputs)
        return result if isinstance(out_shape, list) else result[0]

    chunks = 2
    bins_row = bins.reshape(1, all_bins)
    small = [pltpu.VMEM(v.shape, v.dtype) for v in (bins_row, sensor_coords, grid_coords)]
    spectra, *tables = call(
        transform_kernel,
        [pltpu.VMEM((rows, channel_local), jnp.bfloat16), *small],
        [pltpu.with_memory_space_constraint(v, pltpu.HBM) for v in (bins_row, sensor_coords, grid_coords, series)],
        [
            pltpu.VMEM(series.shape, jnp.bfloat16),
            pltpu.VMEM((rows, channel_local), jnp.float32),
            pltpu.SemaphoreType.DMA((chunks,)),
            pltpu.SemaphoreType.DMA((3,)),
        ],
        near_inputs=False,
    )
    far = {}
    for k in range(1, grid_size // 2):
        far[k] = swap(spectra, "grid", 2 * k)

    def stack(*values):
        return call(stack_kernel, pltpu.VMEM((len(values) * rows, channel_local), jnp.bfloat16), near(*values))

    near_spectra = swap(spectra, "grid", 1)
    corner = swap(spectra, "grid", 3)
    late = [k for k in far if k != 1]
    beam_type = pltpu.VMEM((half, 2, channels, grid_local), jnp.bfloat16)
    squares_type = pltpu.VMEM((channels, grid_local), jnp.float32)
    rates_type = pltpu.VMEM((half, STEP, grid_local), jnp.float32)
    beam0, squares = call(
        functools.partial(replica_kernel, range(FIRST), samples, True),
        [pltpu.VMEM((FIRST, 2, channels, grid_local), jnp.bfloat16), squares_type], near(*tables), [rates_type],
    )
    rest = swap(stack(*[far[k] for k in late]), "grid", 1)
    beam1 = call(
        functools.partial(replica_kernel, range(FIRST, all_bins), samples, False),
        pltpu.VMEM((all_bins - FIRST, 2, channels, grid_local), jnp.bfloat16), near(*tables, squares), [pltpu.VMEM((all_bins - FIRST, STEP, grid_local), jnp.float32)],
    )
    sums = call(
        functools.partial(product_kernel, [[0], *[[2 * k] for k in far], [1], [3]], False),
        pltpu.VMEM((all_bins, 2, 2 * snap_local, grid_local), jnp.float32),
        near(spectra, *far.values(), near_spectra, corner, beam0, beam1),
    )
    total = call(
        functools.partial(product_kernel, [[2 * k + 1 for k in late]], True),
        pltpu.VMEM((all_bins, grid_local), jnp.float32),
        near(rest, beam0, beam1, sums),
    )
    step = freq_size // 2
    while step > 2:
        total += swap(total, "freq", step)
        step //= 2
    others = []
    for mask in (2, 3, 1):
        others.append(swap(total, "freq", mask))
    bin_power, power = call(
        functools.partial(finish_kernel, snap_total),
        [
            jax.ShapeDtypeStruct((all_bins // freq_size, grid_local), jnp.float32),
            jax.ShapeDtypeStruct((1, grid_local), jnp.float32),
        ],
        near(total, *others),
        [pltpu.VMEM((all_bins, grid_local), jnp.float32)],
    )
    return (bin_power, power.reshape(grid_local))


FIRST = 1


def solution(mesh):
    return jax.shard_map(
        on_device,
        mesh=mesh,
        in_specs=(P("freq", "grid", None), P(), P(), P(None, "grid")),
        out_specs=(P("freq", "grid"), P("grid")),
        check_vma=False,
    )
```

```python
import functools
import math

import jax
import jax.numpy as jnp
from jax import lax
from jax.experimental import pallas as pl
from jax.experimental.pallas import tpu as pltpu
from jax.sharding import PartitionSpec as P


def fit(function, degree):
    import numpy as np

    nodes = 0.125 + 0.125 * np.cos(math.pi * (np.arange(degree + 1) + 0.5) / (degree + 1))
    matrix = np.vander(nodes, degree + 1, increasing=True)
    return [float(v) for v in np.linalg.solve(matrix, function(np.sqrt(nodes)))]


def half_sine():
    import numpy as np

    return fit(lambda x: np.sin(math.pi * x) / x, 4)


def horner(u, coefficients):
    total = coefficients[-1]
    for value in coefficients[-2::-1]:
        total = total * u + value
    return total


def scaled_cos_sin(turns, scale):
    whole = (turns + 12582912.0) - 12582912.0
    x = turns - whole
    root = math.sqrt(2.0 * scale)
    s = x * horner(x * x, [-v * root for v in half_sine()])
    real = scale - s * s
    rest = jnp.maximum(real + scale, 1e-30)
    return real, s * (rest * lax.rsqrt(rest))


def features(sensors_ref, places):
    channels, points = sensors_ref.shape[1], places[0].shape[1]
    sensors = [sensors_ref[pl.ds(a, 1), :].astype(jnp.float32) for a in range(3)]
    s_high, s_low = split(sum(v * v for v in sensors))
    g_high, g_low = split(sum(v * v for v in places))
    one = jnp.ones((1, channels), jnp.float32)
    left = jnp.concatenate([-2.0 * v for v in sensors] + [s_high, s_low, 64.0 * one, one, 0.0 * one], 0)
    one = jnp.ones((1, points), jnp.float32)
    right = jnp.concatenate(places + [64.0 * one, one, g_high, g_low, 0.0 * one], 0)
    return left.T.astype(jnp.bfloat16), right.astype(jnp.bfloat16)


def squared(left, right):
    return lax.dot_general(left, right, (((1,), (0,)), ((), ())), preferred_element_type=jnp.float32)


STEP = 128
TOGETHER = 1


def fill(beam_ref, squares, rates):
    channels = squares.shape[0]
    scale = channels ** (-0.5)
    together = TOGETHER if channels % (STEP * TOGETHER) == 0 else 1

    @pl.loop(0, channels // (STEP * together))
    def _(i):
        for part in range(together):
            span = pl.ds(pl.multiple_of((i * together + part) * STEP, STEP), STEP)
            square = squares[span, :]
            distance = square * lax.rsqrt(jnp.maximum(square, 1.0))
            for f in range(beam_ref.shape[0]):
                real, imag = scaled_cos_sin(distance * rates[f], scale)
                beam_ref[f, 0, span, :] = real.astype(jnp.bfloat16)
                beam_ref[f, 1, span, :] = imag.astype(jnp.bfloat16)


def bin_at(bins_ref, f):
    return bins_ref[:, f : f + 1].astype(jnp.float32)


def transform_kernel(
    bins_far, sensors_far, points_far, series_ref, spectra_ref, bins_ref, sensors_ref, points_ref, held, tall, sems, small_sems
):
    snaps, channels, samples = held.shape
    rows = tall.shape[0] // snaps
    all_bins = rows // 2
    chunks = sems.shape[0]
    step = snaps // chunks
    copies = [
        pltpu.make_async_copy(series_ref.at[pl.ds(i * step, step)], held.at[pl.ds(i * step, step)], sems.at[i])
        for i in range(chunks)
    ]
    small = [
        pltpu.make_async_copy(a, b, small_sems.at[i])
        for i, (a, b) in enumerate([(bins_far, bins_ref), (sensors_far, sensors_ref), (points_far, points_ref)])
    ]
    for copy in small:
        copy.start()
    for copy in copies:
        copy.start(priority=1)
    small[0].wait()
    row = lax.broadcasted_iota(jnp.int32, (rows, samples), 0)
    sample = lax.broadcasted_iota(jnp.int32, (rows, samples), 1)
    number = jnp.zeros((rows, samples), jnp.float32)
    for f in range(all_bins):
        number = jnp.where(row // 2 == f, bin_at(bins_ref, f), number)
    turns = number * sample.astype(jnp.float32) * (1.0 / samples)
    cosine, sine = scaled_cos_sin(turns, (samples / 2.0) ** (-0.5))
    table = jnp.where(row % 2 == 0, cosine, sine).astype(jnp.bfloat16)
    group = 2 if channels % 128 == 0 and step % 2 == 0 else 1
    for i, copy in enumerate(copies):
        copy.wait()
        for s in range(i * step, (i + 1) * step, group):
            block = held[s : s + group].reshape(group * channels, samples)
            out = lax.dot_general(table, block, (((1,), (1,)), ((), ())), preferred_element_type=jnp.float32)
            for p in range(group):
                tall[pl.ds((s + p) * rows, rows), :] = out[:, p * channels : (p + 1) * channels]
    for copy in small[1:]:
        copy.wait()
    for k in range(rows):
        picked = tall[pl.ds(k, snaps, stride=rows), :].astype(jnp.bfloat16)
        spectra_ref[pl.ds(k * snaps, snaps), :] = picked


def stack_kernel(*refs):
    out = refs[-1]
    for k, ref in enumerate(refs[:-1]):
        out[pl.ds(k * ref.shape[0], ref.shape[0]), :] = ref[...]


def split(value):
    high = jnp.floor(value * (1.0 / 64.0))
    return high, value - 64.0 * high


def replica_kernel(bins, samples, first, bins_ref, sensors_ref, points_ref, *refs):
    if first:
        beam_ref, squares, rates = refs
        places = [points_ref[pl.ds(a, 1), :].astype(jnp.float32) for a in range(3)]
        squares[...] = squared(*features(sensors_ref, places))
    else:
        squares, beam_ref, rates = refs
    for i, f in enumerate(bins):
        rates[i] = jnp.broadcast_to(bin_at(bins_ref, f) * (2.0 / samples), rates.shape[1:])
    fill(beam_ref, squares, rates)


def product_kernel(masks, last, *refs):
    blocks, beams, rest = refs[: len(masks)], refs[len(masks) : len(masks) + 2], refs[len(masks) + 2 :]
    out = rest[-1]
    sums = rest[0] if last else out
    place = lax.axis_index("grid")
    counts = [beam.shape[0] for beam in beams]
    bins = sum(counts)
    depth = blocks[0].shape[1]
    rows = sums.shape[2]
    snaps = rows // 2
    for f in range(bins):
        beam, at = (beams[0], f) if f < counts[0] else (beams[1], f - counts[0])
        totals = []
        for part in range(2):
            total = rest[0][f, part] if last else None
            for block, inside in zip(blocks, masks):
                for i, mask in enumerate(inside):
                    start = pl.multiple_of((place ^ mask) * depth, depth)
                    term = jnp.dot(
                        block[pl.ds((i * bins + f) * rows, rows), :], beam[at, part, pl.ds(start, depth), :],
                        preferred_element_type=jnp.float32,
                    )
                    total = term if total is None else total + term
            totals.append(total)
        if last:
            real = totals[0][:snaps] + totals[1][snaps:]
            imag = totals[0][snaps:] - totals[1][:snaps]
            out[pl.ds(f, 1), :] = jnp.sum(real * real + imag * imag, 0, keepdims=True)
        else:
            for part in range(2):
                out[f, part] = totals[part]


def vmem(n):
    return [pl.BlockSpec(memory_space=pltpu.VMEM)] * n


def grant(mib):
    return pltpu.CompilerParams(vmem_limit_bytes=mib << 20)


def near(*values):
    return [pltpu.with_memory_space_constraint(v, pltpu.VMEM) for v in values]


def finish_kernel(snap_total, mine_ref, second_ref, third_ref, fourth_ref, bin_power_ref, power_ref, total_ref):
    bin_count = bin_power_ref.shape[0]
    total_ref[...] = ((mine_ref[...] + second_ref[...]) + (third_ref[...] + fourth_ref[...])) / snap_total
    bin_power_ref[...] = total_ref[pl.ds(lax.axis_index("freq") * bin_count, bin_count), :]
    power_ref[...] = jnp.sum(total_ref[...], 0, keepdims=True) / mine_ref.shape[0]


def on_device(series, bins, sensor_coords, grid_coords):
    snap_local, channel_local, samples = series.shape
    all_bins = bins.shape[0]
    channels = sensor_coords.shape[1]
    grid_local = grid_coords.shape[1]
    freq_size = lax.axis_size("freq")
    grid_size = lax.axis_size("grid")
    snap_total = snap_local * freq_size
    half = all_bins // 2
    rows = 2 * all_bins * snap_local

    def swap(value, axis, mask):
        size = lax.axis_size(axis)
        return lax.ppermute(value, axis, [(i, i ^ mask) for i in range(size)])

    def call(kernel, out_shape, inputs, scratch=(), near_inputs=True):
        outs = out_shape if isinstance(out_shape, list) else [out_shape]
        result = pl.pallas_call(
            kernel,
            out_shape=outs,
            in_specs=vmem(len(inputs)) if near_inputs else [pl.BlockSpec(memory_space=pl.ANY)] * len(inputs),
            out_specs=vmem(len(outs)),
            scratch_shapes=scratch,
            compiler_params=grant(12),
        )(*inputs)
        return result if isinstance(out_shape, list) else result[0]

    chunks = 2
    bins_row = bins.reshape(1, all_bins)
    small = [pltpu.VMEM(v.shape, v.dtype) for v in (bins_row, sensor_coords, grid_coords)]
    spectra, *tables = call(
        transform_kernel,
        [pltpu.VMEM((rows, channel_local), jnp.bfloat16), *small],
        [pltpu.with_memory_space_constraint(v, pltpu.HBM) for v in (bins_row, sensor_coords, grid_coords, series)],
        [
            pltpu.VMEM(series.shape, jnp.bfloat16),
            pltpu.VMEM((rows, channel_local), jnp.float32),
            pltpu.SemaphoreType.DMA((chunks,)),
            pltpu.SemaphoreType.DMA((3,)),
        ],
        near_inputs=False,
    )
    far = {}
    for k in range(1, grid_size // 2):
        far[k] = swap(spectra, "grid", 2 * k)

    def stack(*values):
        return call(stack_kernel, pltpu.VMEM((len(values) * rows, channel_local), jnp.bfloat16), near(*values))

    near_spectra = swap(spectra, "grid", 1)
    corner = swap(spectra, "grid", 3)
    late = [k for k in far if k != 1]
    beam_type = pltpu.VMEM((half, 2, channels, grid_local), jnp.bfloat16)
    squares_type = pltpu.VMEM((channels, grid_local), jnp.float32)
    rates_type = pltpu.VMEM((half, STEP, grid_local), jnp.float32)
    beam0, squares = call(
        functools.partial(replica_kernel, range(FIRST), samples, True),
        [pltpu.VMEM((FIRST, 2, channels, grid_local), jnp.bfloat16), squares_type], near(*tables), [rates_type],
    )
    rest = swap(stack(*[far[k] for k in late]), "grid", 1)
    beam1 = call(
        functools.partial(replica_kernel, range(FIRST, all_bins), samples, False),
        pltpu.VMEM((all_bins - FIRST, 2, channels, grid_local), jnp.bfloat16), near(*tables, squares), [pltpu.VMEM((all_bins - FIRST, STEP, grid_local), jnp.float32)],
    )
    sums = call(
        functools.partial(product_kernel, [[0], *[[2 * k] for k in far], [1], [3]], False),
        pltpu.VMEM((all_bins, 2, 2 * snap_local, grid_local), jnp.float32),
        near(spectra, *far.values(), near_spectra, corner, beam0, beam1),
    )
    total = call(
        functools.partial(product_kernel, [[2 * k + 1 for k in late]], True),
        pltpu.VMEM((all_bins, grid_local), jnp.float32),
        near(rest, beam0, beam1, sums),
    )
    step = freq_size // 2
    while step > 2:
        total += swap(total, "freq", step)
        step //= 2
    others = []
    for mask in (2, 3, 1):
        others.append(swap(total, "freq", mask))
    bin_power, power = call(
        functools.partial(finish_kernel, snap_total),
        [
            jax.ShapeDtypeStruct((all_bins // freq_size, grid_local), jnp.float32),
            jax.ShapeDtypeStruct((1, grid_local), jnp.float32),
        ],
        near(total, *others),
        [pltpu.VMEM((all_bins, grid_local), jnp.float32)],
    )
    return (bin_power, power.reshape(grid_local))


FIRST = 1


def solution(mesh):
    return jax.shard_map(
        on_device,
        mesh=mesh,
        in_specs=(P("freq", "grid", None), P(), P(), P(None, "grid")),
        out_specs=(P("freq", "grid"), P("grid")),
        check_vma=False,
    )
```
